512 devices in a mesh: dp: 16 (over y, core), tensor: 32 (over z, x).
Axes of the slice: x: 4, y: 8, z: 8, core: 2. Of those that a mesh axis runs over, the one named last changes fastest.
Arguments:
- tokens: bfloat16 [5632, 4096], P('dp', 'tensor'), may hold values from -6 to 6
- grad_out: bfloat16 [5632, 4096], P('dp', 'tensor'), may hold values from -6 to 6
- routes: float32 [16, 2, 16], P('dp'), may hold values from 0.005 to 0.3
- counts: int32 [16], P('dp'), may hold values from 176 to 352
- up_weight: bfloat16 [16, 4096, 4096], P(None, 'dp', 'tensor'), may hold values from -0.09375 to 0.09375
- down_weight: bfloat16 [16, 4096, 4096], P(None, 'tensor', 'dp'), may hold values from -0.09375 to 0.09375
Outputs:
- input_grad: bfloat16 [5632, 4096], P('dp', 'tensor')
- up_grad: bfloat16 [16, 4096, 4096], P(None, 'dp', 'tensor')
- down_grad: bfloat16 [16, 4096, 4096], P(None, 'tensor', 'dp')
- route_grad: float32 [16, 2, 16], P('dp')
The draws below stay inside these ranges and needn't reach their ends.
Inputs may be any that keep to these rules, and one draw needn't show every extreme that they name: `counts`: the valid tokens of a data group, at least one whole segment.
All inputs are finite; a program needn't handle non-finite values.
Results may differ from the reference program's by a relative error of at most 0.02.
Values may be sent and summed in bfloat16 or wider, within the bound.
No kernel may reach another device: no remote copies, remote signals or barrier semaphores. Data moves between devices by JAX's collectives and lax.ppermute only.
A program may use at most 64 MiB of HBM per device.

```python
import math
import jax
import jax.numpy as jnp
from jax import lax

D = 4096
FFN = 4096
EXPERTS = 16
SEGS = 2
SEG_LEN = 176
TOK_GROUP = 352
GROUPS = 16
TOKENS = 5632
N_DP = 16
N_TENSOR = 32


def touch_ends(entries, key, least, high):
    index_at = [jax.random.randint(jax.random.fold_in(key, axis), (), 0, length) for axis, length in enumerate(entries.shape)]
    longest = entries.shape.index(max(entries.shape))
    beside = index_at[:longest] + [(index_at[longest] + 1) % entries.shape[longest]] + index_at[longest + 1:]
    return entries.at[tuple(index_at)].set(least).at[tuple(beside)].set(high)


def level_of(key, extent, pieces, low, high):
    def one(position, shards_of):
        heights = jax.random.uniform(jax.random.fold_in(jax.random.fold_in(key, 6), position), (shards_of,), jnp.float32, low / len(pieces), high / len(pieces))
        return jnp.repeat(jnp.exp(heights), extent[position] // shards_of).reshape((-1,) + (1,) * (len(extent) - position - 1))

    factor_of = one(*pieces[0])
    for cut in pieces[1:]:
        factor_of = factor_of * one(*cut)
    return factor_of


def bell_draw(own_key, extent, scale, limit, split=(), held_as=jnp.bfloat16):
    level = level_of(own_key, extent, split, -0.22, 0.18) if split else 1.0
    values = jax.random.normal(own_key, extent, jnp.float32) * scale * level
    return jnp.minimum(jnp.maximum(values, -limit), limit).astype(held_as)


def setup_inputs(seed: int = 0) -> dict:
    arg_keys = jax.random.split(jax.random.key(seed), 7)
    tokens = bell_draw(arg_keys[0], (TOKENS, D), 1.0, 6.0, ((0, 16), (1, 32)))
    grad_out = bell_draw(arg_keys[1], (TOKENS, D), 1.0, 6.0, ((0, 16), (1, 32)))
    routes = jnp.clip(jnp.exp(math.log(0.3) - 4.0943446 * jax.random.uniform(arg_keys[2], (GROUPS, SEGS, EXPERTS), jnp.float32) ** level_of(arg_keys[2], (GROUPS, SEGS, EXPERTS), ((0, 16),), -0.2, 0.2)), 0.005, 0.3)
    counts = touch_ends(jax.random.randint(arg_keys[3], (GROUPS,), SEG_LEN, TOK_GROUP + 1), jax.random.fold_in(arg_keys[3], 1), SEG_LEN, TOK_GROUP).astype(jnp.int32)
    up_weight = bell_draw(arg_keys[4], (EXPERTS, D, FFN), D ** -0.5, 0.09375, ((1, 16), (2, 32)))
    down_weight = bell_draw(arg_keys[5], (EXPERTS, FFN, D), FFN ** -0.5, 0.09375, ((1, 32), (2, 16)))
    return dict(tokens=tokens, grad_out=grad_out, routes=routes, counts=counts, up_weight=up_weight, down_weight=down_weight)


gelu_scale = 0.7978845608
gelu_cubic = 0.044715


def gelu_pair(inputs):
    inner = gelu_scale * (inputs + gelu_cubic * inputs * inputs * inputs)
    tangent = jnp.tanh(inner)
    activated = 0.5 * inputs * (1.0 + tangent)
    derivative = 0.5 * (1.0 + tangent) + 0.5 * inputs * (1.0 - tangent * tangent) * gelu_scale * (1.0 + 3.0 * gelu_cubic * inputs * inputs)
    return activated, derivative


def reference(tokens, grad_out, routes, counts, up_weight, down_weight):
    experts, width, hidden = up_weight.shape
    segments = routes.shape[1]
    group_rows = tokens.shape[0] // N_DP
    seg_rows = group_rows // segments
    slices = N_TENSOR
    up_flat = up_weight.reshape(experts, -1)
    down_flat = down_weight.reshape(experts, -1)
    up_wide = up_flat.astype(jnp.float32)
    down_wide = down_flat.astype(jnp.float32)
    high = lax.Precision.HIGHEST

    def per_group(carry, group):
        up_acc, down_acc = carry
        start = (group * group_rows).astype(jnp.int32)
        group_tokens = lax.dynamic_slice_in_dim(tokens, start, group_rows, 0)
        group_grads = lax.dynamic_slice_in_dim(grad_out, start, group_rows, 0)
        valid = (jnp.arange(group_rows, dtype=jnp.int32) < counts[group])[:, None]
        group_grads = jnp.where(valid, group_grads, jnp.zeros_like(group_grads))
        weights = routes[group]
        merged_up = jnp.dot(weights, up_wide, precision=high).reshape(segments, width, hidden).astype(jnp.bfloat16)
        merged_down = jnp.dot(weights, down_wide, precision=high).reshape(segments, hidden, width).astype(jnp.bfloat16)
        input_parts = []
        products = []
        for segment in range(segments):
            seg_tokens = group_tokens[segment * seg_rows:(segment + 1) * seg_rows]
            seg_grads = group_grads[segment * seg_rows:(segment + 1) * seg_rows]
            pre = jnp.dot(seg_tokens, merged_up[segment], preferred_element_type=jnp.float32)
            activated, derivative = gelu_pair(pre)
            activated = activated.astype(jnp.bfloat16)
            back = jnp.dot(seg_grads, merged_down[segment].T, preferred_element_type=jnp.float32)
            hidden_grad = (back * derivative).astype(jnp.bfloat16)
            up_term = jnp.dot(seg_tokens.T, hidden_grad, preferred_element_type=jnp.float32).astype(jnp.bfloat16)
            down_term = jnp.dot(activated.T, seg_grads, preferred_element_type=jnp.float32).astype(jnp.bfloat16)
            left_side = hidden_grad.astype(jnp.float32).reshape(seg_rows, slices, hidden // slices)
            right_side = merged_up[segment].astype(jnp.float32).reshape(width, slices, hidden // slices)
            partial_value = jnp.einsum('rth,dth->trd', left_side, right_side, precision=high).astype(jnp.bfloat16)
            partial_value = lax.optimization_barrier(partial_value)
            input_parts.append(jnp.sum(partial_value.astype(jnp.float32), axis=0).astype(jnp.bfloat16))
            up_vector = up_term.reshape(-1)
            down_vector = down_term.reshape(-1)
            up_acc = up_acc + weights[segment][:, None] * up_vector.astype(jnp.float32)[None, :]
            down_acc = down_acc + weights[segment][:, None] * down_vector.astype(jnp.float32)[None, :]
            inner_up = jnp.dot(up_flat, up_vector, preferred_element_type=jnp.float32)
            inner_down = jnp.dot(down_flat, down_vector, preferred_element_type=jnp.float32)
            products.append(inner_up + inner_down)
        return (up_acc, down_acc), (jnp.concatenate(input_parts, axis=0), jnp.stack(products, axis=0))

    start_acc = (jnp.zeros((experts, width * hidden), jnp.float32), jnp.zeros((experts, width * hidden), jnp.float32))
    (up_acc, down_acc), (input_rows, route_rows) = lax.scan(per_group, start_acc, jnp.arange(N_DP, dtype=jnp.int32))
    input_grad = input_rows.reshape(N_DP * group_rows, width)
    up_grad = up_acc.reshape(experts, width, hidden).astype(jnp.bfloat16)
    down_grad = down_acc.reshape(experts, hidden, width).astype(jnp.bfloat16)
    return (input_grad, up_grad, down_grad, route_rows)
```

```python
import functools

import jax
import jax.numpy as jnp
from jax import lax
from jax.experimental import pallas as pl
from jax.experimental.pallas import tpu as pltpu
from jax.sharding import Mesh, PartitionSpec as P

gelu_scale = 0.7978845608
gelu_cubic = 0.044715

DP = ("y", "c")
TENSOR = ("z", "x")


def gelu_pair(inputs):
    inner = gelu_scale * (inputs + gelu_cubic * inputs * inputs * inputs)
    tangent = jnp.tanh(inner)
    activated = 0.5 * inputs * (1.0 + tangent)
    derivative = 0.5 * (1.0 + tangent) + 0.5 * inputs * (1.0 - tangent * tangent) * gelu_scale * (
        1.0 + 3.0 * gelu_cubic * inputs * inputs
    )
    return (activated, derivative)


def dot(lhs, rhs, lhs_dim, rhs_dim):
    return lax.dot_general(
        lhs, rhs, (((lhs_dim,), (rhs_dim,)), ((), ())), preferred_element_type=jnp.float32
    )


def vmem(count):
    return [pl.BlockSpec(memory_space=pltpu.VMEM) for _ in range(count)]


def local_kernel(kernel, out_shapes, scalars, *args):
    smem = [pl.BlockSpec(memory_space=pltpu.SMEM) for _ in range(scalars)]
    return pl.pallas_call(
        kernel,
        out_shape=out_shapes,
        in_specs=smem + vmem(len(args) - scalars),
        out_specs=jax.tree.map(lambda _: vmem(1)[0], out_shapes),
        compiler_params=pltpu.CompilerParams(vmem_limit_bytes=56 * 1024 * 1024),
    )(*args)


def pair(full_ref, i, start, rows):
    return jnp.concatenate(
        [
            full_ref[2 * i, pl.ds(start, rows), :],
            full_ref[2 * i + 1, pl.ds(start, rows), :],
        ],
        axis=1,
    )


def pre_kernel(full_ref, up_ref, act_ref, slope_ref):
    slices, segments = up_ref.shape[0], up_ref.shape[1]
    rows = slope_ref.shape[0] // segments
    for s in range(segments):
        pre = jnp.zeros((rows, slope_ref.shape[1]), jnp.float32)
        for i in range(slices):
            pre = pre + dot(pair(full_ref, i, s * rows, rows), up_ref[i, s], 1, 0)
        activated, derivative = gelu_pair(pre)
        activated = activated.astype(jnp.bfloat16)
        slope_ref[pl.ds(s * rows, rows), :] = derivative
        for copy in range(act_ref.shape[0]):
            act_ref[copy, pl.ds(s * rows, rows), :] = activated


def back_kernel(full_ref, down_ref, slope_ref, hid_ref):
    slices, segments = down_ref.shape[0], down_ref.shape[1]
    group_rows = slope_ref.shape[0]
    rows = group_rows // segments
    for s in range(segments):
        back = jnp.zeros((rows, slope_ref.shape[1]), jnp.float32)
        for i in range(slices):
            back = back + dot(pair(full_ref, i, group_rows + s * rows, rows), down_ref[i, s], 1, 1)
        hidden = (back * slope_ref[pl.ds(s * rows, rows), :]).astype(jnp.bfloat16)
        for copy in range(hid_ref.shape[0]):
            hid_ref[copy, pl.ds(s * rows, rows), :] = hidden


def terms_kernel(which, where_ref, blocks_ref, same_ref, other_ref, out_ref):
    n_x, n_z = blocks_ref.shape[0], blocks_ref.shape[1]
    group_rows = same_ref.shape[1]
    segments = out_ref.shape[0] // (2 * n_z)
    rows = group_rows // segments
    z, x, core = where_ref[0], where_ref[1], where_ref[2]

    def step(g, carry):
        k = lax.rem(z - g + n_z, n_z)
        for c in range(2):
            low = lax.rem(x - 2 * c + n_x, n_x)
            high = lax.rem(x - 2 * c - 1 + n_x, n_x)
            for s in range(segments):
                own = pl.ds(s * rows, rows)
                rows_at = pl.ds(which * group_rows + s * rows, rows)
                block = jnp.concatenate(
                    [blocks_ref[low, k, rows_at, :], blocks_ref[high, k, rows_at, :]], axis=1
                )
                side = jnp.where(core == c, same_ref[g, own, :], other_ref[g, own, :])
                term = dot(side, block, 0, 0) if which else dot(block, side, 0, 0)
                out_ref[(2 * g + c) * segments + s] = term.astype(jnp.bfloat16)
        return carry

    lax.fori_loop(0, n_z, step, 0)


def input_kernel(where_ref, hid_ref, up_ref, out_ref):
    slices, segments = up_ref.shape[0], up_ref.shape[1]
    n_x, n_z, group_rows = out_ref.shape[0], out_ref.shape[1], out_ref.shape[2]
    rows = group_rows // segments
    z, x = where_ref[0], where_ref[1]
    for s in range(segments):
        hidden = hid_ref[0, pl.ds(s * rows, rows), :]
        for i in range(slices):
            part = dot(hidden, up_ref[i, s], 1, 1).astype(jnp.bfloat16)
            for half in range(2):
                t = 2 * i + half
                to_x = lax.rem(t % n_x - x + n_x, n_x)
                to_z = lax.rem(t // n_x - z + n_z, n_z)
                out_ref[to_x, to_z, pl.ds(s * rows, rows), :] = part[
                    :, half * 128 : (half + 1) * 128
                ]


def exchange(value, axes):
    return lax.all_to_all(value, axes, split_axis=0, concat_axis=0, tiled=True)


def shift(value, axis, by):
    size = lax.axis_size(axis)
    return lax.ppermute(value, axis, [(i, (i + by) % size) for i in range(size)])


def add(*values):
    return functools.reduce(lambda a, b: a + b, [v.astype(jnp.float32) for v in values])


def turn(value):
    n_dp = lax.axis_size("y") * lax.axis_size("c")
    n_t = lax.axis_size("z") * lax.axis_size("x")
    moves = [
        (g * n_t + t, (t // 2) * n_t + 2 * g + t % 2) for g in range(n_dp) for t in range(n_t)
    ]
    return lax.ppermute(value, DP + TENSOR, moves)


def scatter_sum(parts):
    n_z = parts.shape[1]
    half = n_z // 2
    bf16 = jnp.bfloat16
    from_left = shift(parts[2, :half], "x", 1)
    from_right = shift(parts[2, half:], "x", -1)
    right = jnp.concatenate([add(parts[1, :half], from_left).astype(bf16), parts[1, half:]])
    left = jnp.concatenate([parts[3, :half], add(parts[3, half:], from_right).astype(bf16)])
    near = add(parts[0], shift(right, "x", 1), shift(left, "x", -1)).astype(bf16)
    return add(near[0], *[shift(near[k], "z", k) for k in range(1, n_z)]).astype(bf16)


def body(tokens, grad_out, routes, counts, up_weight, down_weight):
    group_rows, lanes = tokens.shape
    experts, width, hidden = up_weight.shape
    segments = routes.shape[1]
    high = lax.Precision.HIGHEST
    n_y = lax.axis_size("y")
    n_dp = n_y * lax.axis_size("c")
    n_z, n_x = lax.axis_size("z"), lax.axis_size("x")
    bf16 = jnp.bfloat16
    shape = jax.ShapeDtypeStruct
    here = jnp.stack([lax.axis_index(a).astype(jnp.int32) for a in ("z", "x", "c")])
    routes_out = jnp.broadcast_to(routes, (n_dp,) + routes.shape[1:])
    all_routes = exchange(routes_out, DP)
    flat_routes = all_routes.reshape(-1, experts)
    valid = (jnp.arange(group_rows, dtype=jnp.int32) < counts[0])[:, None]
    masked = jnp.where(valid, grad_out, jnp.zeros_like(grad_out))
    both = jnp.concatenate([tokens, masked], axis=0)
    turned = turn(both)
    full = lax.all_gather(both, TENSOR)
    local_up = jnp.einsum(
        "ke,edh->kdh", flat_routes, up_weight.astype(jnp.float32), precision=high
    ).astype(bf16)
    local_up, turned = lax.optimization_barrier((local_up, turned))
    merged_up = exchange(local_up, DP).reshape(n_dp, segments, width, hidden)
    local_down = jnp.einsum(
        "ke,ehd->khd", flat_routes, down_weight.astype(jnp.float32), precision=high
    ).astype(bf16)
    near = jnp.stack([turned] + [shift(turned, "z", k) for k in range(1, n_z)])
    local_down, near = lax.optimization_barrier((local_down, near))
    merged_down = exchange(local_down, DP).reshape(n_dp, segments, hidden, width)
    right = shift(near, "x", 1)
    left = shift(near, "x", -1)
    merged_down, right, left = lax.optimization_barrier((merged_down, right, left))
    half = n_z // 2
    far = jnp.concatenate([shift(right[:half], "x", 1), shift(left[half:], "x", -1)], axis=0)
    blocks = jnp.stack([near, right, far, left])

    copies = shape((n_y, group_rows, hidden), bf16)
    act, slope = local_kernel(
        pre_kernel, (copies, shape((group_rows, hidden), jnp.float32)), 0, full, merged_up
    )
    hid = local_kernel(back_kernel, copies, 0, full, merged_down, slope)
    act_same = exchange(act, "y")
    act_other = shift(act_same, "c", 1)
    hid_same = exchange(hid, "y")
    parts = local_kernel(
        input_kernel, shape((n_x, n_z, group_rows, lanes), bf16), 1, here, hid, merged_up
    )
    summed = scatter_sum(parts)
    down_terms = local_kernel(
        functools.partial(terms_kernel, 1),
        shape((n_dp * segments, hidden, width), bf16),
        1,
        here,
        blocks,
        act_same,
        act_other,
    )
    down_grad = jnp.einsum(
        "ke,khd->ehd", flat_routes, down_terms.astype(jnp.float32), precision=high
    ).astype(bf16)
    down_inner = jnp.einsum(
        "khd,ehd->ke", down_terms, down_weight, preferred_element_type=jnp.float32
    )
    hid_same, down_grad, down_inner = lax.optimization_barrier((hid_same, down_grad, down_inner))
    hid_other = shift(hid_same, "c", 1)
    up_terms = local_kernel(
        functools.partial(terms_kernel, 0),
        shape((n_dp * segments, width, hidden), bf16),
        1,
        here,
        blocks,
        hid_same,
        hid_other,
    )
    up_grad = jnp.einsum(
        "ke,kdh->edh", flat_routes, up_terms.astype(jnp.float32), precision=high
    ).astype(bf16)
    inner = down_inner + jnp.einsum(
        "kdh,edh->ke", up_terms, up_weight, preferred_element_type=jnp.float32
    )
    own = jnp.sum(exchange(inner.reshape(all_routes.shape), DP), axis=0)
    pieces = exchange(jnp.broadcast_to(own[None], (n_z * n_x,) + own.shape), TENSOR)
    route_grad = jnp.sum(pieces, axis=0)[None]
    return (summed, up_grad, down_grad, route_grad)


def solution(mesh):
    fine = Mesh(mesh.devices.reshape(8, 2, 8, 4), DP + TENSOR)
    return jax.shard_map(
        body,
        mesh=fine,
        in_specs=(
            P(DP, TENSOR),
            P(DP, TENSOR),
            P(DP, None, None),
            P(DP),
            P(None, DP, TENSOR),
            P(None, TENSOR, DP),
        ),
        out_specs=(
            P(DP, TENSOR),
            P(None, DP, TENSOR),
            P(None, TENSOR, DP),
            P(DP, None, None),
        ),
        check_vma=False,
    )
```

```python
import functools

import jax
import jax.numpy as jnp
from jax import lax
from jax.experimental import pallas as pl
from jax.experimental.pallas import tpu as pltpu
from jax.sharding import Mesh, PartitionSpec as P

gelu_scale = 0.7978845608
gelu_cubic = 0.044715

DP = ("y", "c")
TENSOR = ("z", "x")


def gelu_pair(inputs):
    inner = gelu_scale * (inputs + gelu_cubic * inputs * inputs * inputs)
    tangent = jnp.tanh(inner)
    activated = 0.5 * inputs * (1.0 + tangent)
    derivative = 0.5 * (1.0 + tangent) + 0.5 * inputs * (1.0 - tangent * tangent) * gelu_scale * (
        1.0 + 3.0 * gelu_cubic * inputs * inputs
    )
    return (activated, derivative)


def dot(lhs, rhs, lhs_dim, rhs_dim):
    return lax.dot_general(
        lhs, rhs, (((lhs_dim,), (rhs_dim,)), ((), ())), preferred_element_type=jnp.float32
    )


def vmem(count):
    return [pl.BlockSpec(memory_space=pltpu.VMEM) for _ in range(count)]


def local_kernel(kernel, out_shapes, scalars, *args):
    smem = [pl.BlockSpec(memory_space=pltpu.SMEM) for _ in range(scalars)]
    return pl.pallas_call(
        kernel,
        out_shape=out_shapes,
        in_specs=smem + vmem(len(args) - scalars),
        out_specs=jax.tree.map(lambda _: vmem(1)[0], out_shapes),
        compiler_params=pltpu.CompilerParams(vmem_limit_bytes=56 * 1024 * 1024),
    )(*args)


def pair(full_ref, i, start, rows):
    return jnp.concatenate(
        [
            full_ref[2 * i, pl.ds(start, rows), :],
            full_ref[2 * i + 1, pl.ds(start, rows), :],
        ],
        axis=1,
    )


def pre_kernel(full_ref, up_ref, slope_ref, term_ref):
    slices, segments = up_ref.shape[0], up_ref.shape[1]
    group_rows = slope_ref.shape[0]
    rows = group_rows // segments
    for s in range(segments):
        pre = jnp.zeros((rows, slope_ref.shape[1]), jnp.float32)
        for i in range(slices):
            pre = pre + dot(pair(full_ref, i, s * rows, rows), up_ref[i, s], 1, 0)
        activated, derivative = gelu_pair(pre)
        activated = activated.astype(jnp.bfloat16)
        slope_ref[pl.ds(s * rows, rows), :] = derivative
        for i in range(slices):
            term_ref[i, s] = dot(
                activated, pair(full_ref, i, group_rows + s * rows, rows), 0, 0
            ).astype(jnp.bfloat16)


def back_kernel(full_ref, down_ref, slope_ref, hid_ref, term_ref):
    slices, segments = down_ref.shape[0], down_ref.shape[1]
    group_rows = slope_ref.shape[0]
    rows = group_rows // segments
    for s in range(segments):
        back = jnp.zeros((rows, slope_ref.shape[1]), jnp.float32)
        for i in range(slices):
            back = back + dot(pair(full_ref, i, group_rows + s * rows, rows), down_ref[i, s], 1, 1)
        hidden = (back * slope_ref[pl.ds(s * rows, rows), :]).astype(jnp.bfloat16)
        hid_ref[pl.ds(s * rows, rows), :] = hidden
        for i in range(slices):
            term_ref[i, s] = dot(pair(full_ref, i, s * rows, rows), hidden, 0, 0).astype(
                jnp.bfloat16
            )


def input_kernel(where_ref, hid_ref, up_ref, out_ref):
    slices, segments = up_ref.shape[0], up_ref.shape[1]
    n_x, n_z, group_rows = out_ref.shape[0], out_ref.shape[1], out_ref.shape[2]
    rows = group_rows // segments
    z, x = where_ref[0], where_ref[1]
    for s in range(segments):
        hidden = hid_ref[pl.ds(s * rows, rows), :]
        for i in range(slices):
            part = dot(hidden, up_ref[i, s], 1, 1).astype(jnp.bfloat16)
            for half in range(2):
                t = 2 * i + half
                to_x = lax.rem(t % n_x - x + n_x, n_x)
                to_z = lax.rem(t // n_x - z + n_z, n_z)
                out_ref[to_x, to_z, pl.ds(s * rows, rows), :] = part[
                    :, half * 128 : (half + 1) * 128
                ]


def exchange(value, axes):
    return lax.all_to_all(value, axes, split_axis=0, concat_axis=0, tiled=True)


def shift(value, axis, by):
    size = lax.axis_size(axis)
    return lax.ppermute(value, axis, [(i, (i + by) % size) for i in range(size)])


def add(*values):
    return functools.reduce(lambda a, b: a + b, [v.astype(jnp.float32) for v in values])


def start_sum(parts):
    half = parts.shape[1] // 2
    bf16 = jnp.bfloat16
    from_left = shift(parts[2, :half], "x", 1)
    from_right = shift(parts[2, half:], "x", -1)
    right = jnp.concatenate([add(parts[1, :half], from_left).astype(bf16), parts[1, half:]])
    left = jnp.concatenate([parts[3, :half], add(parts[3, half:], from_right).astype(bf16)])
    return right, left


def finish_sum(own, right, left):
    bf16 = jnp.bfloat16
    near = add(own, shift(right, "x", 1), shift(left, "x", -1)).astype(bf16)
    hops = [shift(near[k], "z", k) for k in range(1, near.shape[0])]
    return add(near[0], *hops).astype(bf16)


def body(tokens, grad_out, routes, counts, up_weight, down_weight):
    group_rows, lanes = tokens.shape
    experts, width, hidden = up_weight.shape
    segments = routes.shape[1]
    high = lax.Precision.HIGHEST
    n_y = lax.axis_size("y")
    n_dp = n_y * lax.axis_size("c")
    n_z, n_x = lax.axis_size("z"), lax.axis_size("x")
    bf16 = jnp.bfloat16
    shape = jax.ShapeDtypeStruct
    here = jnp.stack([lax.axis_index(a).astype(jnp.int32) for a in ("z", "x")])
    routes_out = jnp.broadcast_to(routes, (n_dp,) + routes.shape[1:])
    all_routes = exchange(routes_out, DP)
    flat_routes = all_routes.reshape(-1, experts)
    valid = (jnp.arange(group_rows, dtype=jnp.int32) < counts[0])[:, None]
    masked = jnp.where(valid, grad_out, jnp.zeros_like(grad_out))
    both = jnp.concatenate([tokens, masked], axis=0)
    full = lax.all_gather(both, TENSOR)
    local_up = jnp.einsum(
        "ke,edh->kdh", flat_routes, up_weight.astype(jnp.float32), precision=high
    ).astype(bf16)
    merged_up = exchange(local_up, DP).reshape(n_dp, segments, width, hidden)
    local_down = jnp.einsum(
        "ke,ehd->khd", flat_routes, down_weight.astype(jnp.float32), precision=high
    ).astype(bf16)
    merged_down = exchange(local_down, DP).reshape(n_dp, segments, hidden, width)

    slope, down_terms = local_kernel(
        pre_kernel,
        (
            shape((group_rows, hidden), jnp.float32),
            shape((n_dp, segments, hidden, width), bf16),
        ),
        0,
        full,
        merged_up,
    )
    down_terms = exchange(down_terms.reshape(-1, hidden, width), DP)
    hid, up_terms = local_kernel(
        back_kernel,
        (shape((group_rows, hidden), bf16), shape((n_dp, segments, width, hidden), bf16)),
        0,
        full,
        merged_down,
        slope,
    )
    parts = local_kernel(
        input_kernel, shape((n_x, n_z, group_rows, lanes), bf16), 1, here, hid, merged_up
    )
    right, left = start_sum(parts)
    up_terms, right, left = lax.optimization_barrier((up_terms, right, left))
    summed = finish_sum(parts[0], right, left)
    down_grad = jnp.einsum(
        "ke,khd->ehd", flat_routes, down_terms.astype(jnp.float32), precision=high
    ).astype(bf16)
    down_inner = jnp.einsum(
        "khd,ehd->ke", down_terms, down_weight, preferred_element_type=jnp.float32
    )
    up_terms = exchange(up_terms.reshape(-1, width, hidden), DP)
    up_terms, down_grad, down_inner, summed = lax.optimization_barrier(
        (up_terms, down_grad, down_inner, summed)
    )
    up_grad = jnp.einsum(
        "ke,kdh->edh", flat_routes, up_terms.astype(jnp.float32), precision=high
    ).astype(bf16)
    inner = down_inner + jnp.einsum(
        "kdh,edh->ke", up_terms, up_weight, preferred_element_type=jnp.float32
    )
    own = jnp.sum(exchange(inner.reshape(all_routes.shape), DP), axis=0)
    pieces = exchange(jnp.broadcast_to(own[None], (n_z * n_x,) + own.shape), TENSOR)
    route_grad = jnp.sum(pieces, axis=0)[None]
    return (summed, up_grad, down_grad, route_grad)


def solution(mesh):
    fine = Mesh(mesh.devices.reshape(8, 2, 8, 4), DP + TENSOR)
    return jax.shard_map(
        body,
        mesh=fine,
        in_specs=(
            P(DP, TENSOR),
            P(DP, TENSOR),
            P(DP, None, None),
            P(DP),
            P(None, DP, TENSOR),
            P(None, TENSOR, DP),
        ),
        out_specs=(
            P(DP, TENSOR),
            P(None, DP, TENSOR),
            P(None, TENSOR, DP),
            P(DP, None, None),
        ),
        check_vma=False,
    )
```

```python
import functools

import jax
import jax.numpy as jnp
from jax import lax
from jax.experimental import pallas as pl
from jax.experimental.pallas import tpu as pltpu
from jax.sharding import Mesh, PartitionSpec as P

gelu_scale = 0.7978845608
gelu_cubic = 0.044715

DP = ("y", "c")
TENSOR = ("z", "x")


def gelu_pair(inputs):
    inner = gelu_scale * (inputs + gelu_cubic * inputs * inputs * inputs)
    tangent = jnp.tanh(inner)
    activated = 0.5 * inputs * (1.0 + tangent)
    derivative = 0.5 * (1.0 + tangent) + 0.5 * inputs * (1.0 - tangent * tangent) * gelu_scale * (
        1.0 + 3.0 * gelu_cubic * inputs * inputs
    )
    return (activated, derivative)


def dot(lhs, rhs, lhs_dim, rhs_dim):
    return lax.dot_general(
        lhs, rhs, (((lhs_dim,), (rhs_dim,)), ((), ())), preferred_element_type=jnp.float32
    )


def vmem(count):
    return [pl.BlockSpec(memory_space=pltpu.VMEM) for _ in range(count)]


def local_kernel(kernel, out_shapes, scalars, *args):
    smem = [pl.BlockSpec(memory_space=pltpu.SMEM) for _ in range(scalars)]
    return pl.pallas_call(
        kernel,
        out_shape=out_shapes,
        in_specs=smem + vmem(len(args) - scalars),
        out_specs=jax.tree.map(lambda _: vmem(1)[0], out_shapes),
        compiler_params=pltpu.CompilerParams(vmem_limit_bytes=56 * 1024 * 1024),
    )(*args)


def pair(full_ref, i, start, rows):
    return jnp.concatenate(
        [
            full_ref[2 * i, pl.ds(start, rows), :],
            full_ref[2 * i + 1, pl.ds(start, rows), :],
        ],
        axis=1,
    )


def pre_kernel(full_ref, up_ref, slope_ref, term_ref):
    slices, segments = up_ref.shape[0], up_ref.shape[1]
    group_rows = slope_ref.shape[0]
    rows = group_rows // segments
    for s in range(segments):
        pre = jnp.zeros((rows, slope_ref.shape[1]), jnp.float32)
        for i in range(slices):
            pre = pre + dot(pair(full_ref, i, s * rows, rows), up_ref[i, s], 1, 0)
        activated, derivative = gelu_pair(pre)
        activated = activated.astype(jnp.bfloat16)
        slope_ref[pl.ds(s * rows, rows), :] = derivative
        for i in range(slices):
            term_ref[i, s] = dot(
                activated, pair(full_ref, i, group_rows + s * rows, rows), 0, 0
            ).astype(jnp.bfloat16)


def back_kernel(full_ref, down_ref, slope_ref, hid_ref, term_ref):
    slices, segments = down_ref.shape[0], down_ref.shape[1]
    group_rows = slope_ref.shape[0]
    rows = group_rows // segments
    for s in range(segments):
        back = jnp.zeros((rows, slope_ref.shape[1]), jnp.float32)
        for i in range(slices):
            back = back + dot(pair(full_ref, i, group_rows + s * rows, rows), down_ref[i, s], 1, 1)
        hidden = (back * slope_ref[pl.ds(s * rows, rows), :]).astype(jnp.bfloat16)
        hid_ref[pl.ds(s * rows, rows), :] = hidden
        for i in range(slices):
            term_ref[i, s] = dot(pair(full_ref, i, s * rows, rows), hidden, 0, 0).astype(
                jnp.bfloat16
            )


def input_kernel(where_ref, hid_ref, up_ref, out_ref):
    slices, segments = up_ref.shape[0], up_ref.shape[1]
    n_x, n_z, group_rows = out_ref.shape[0], out_ref.shape[1], out_ref.shape[2]
    rows = group_rows // segments
    z, x = where_ref[0], where_ref[1]
    for s in range(segments):
        hidden = hid_ref[pl.ds(s * rows, rows), :]
        for i in range(slices):
            part = dot(hidden, up_ref[i, s], 1, 1).astype(jnp.bfloat16)
            for half in range(2):
                t = 2 * i + half
                to_x = lax.rem(t % n_x - x + n_x, n_x)
                to_z = lax.rem(t // n_x - z + n_z, n_z)
                out_ref[to_x, to_z, pl.ds(s * rows, rows), :] = part[
                    :, half * 128 : (half + 1) * 128
                ]


def exchange(value, axes):
    return lax.all_to_all(value, axes, split_axis=0, concat_axis=0, tiled=True)


def shift(value, axis, by):
    size = lax.axis_size(axis)
    return lax.ppermute(value, axis, [(i, (i + by) % size) for i in range(size)])


def add(*values):
    return functools.reduce(lambda a, b: a + b, [v.astype(jnp.float32) for v in values])


def start_sum(parts):
    half = parts.shape[1] // 2
    bf16 = jnp.bfloat16
    from_left = shift(parts[2, :half], "x", 1)
    from_right = shift(parts[2, half:], "x", -1)
    right = jnp.concatenate([add(parts[1, :half], from_left).astype(bf16), parts[1, half:]])
    left = jnp.concatenate([parts[3, :half], add(parts[3, half:], from_right).astype(bf16)])
    return right, left


def second_hop(own, right, left):
    return add(own, shift(right, "x", 1), shift(left, "x", -1)).astype(jnp.bfloat16)


def finish_sum(near):
    hops = [shift(near[k], "z", k) for k in range(1, near.shape[0])]
    return add(near[0], *hops).astype(jnp.bfloat16)


def body(tokens, grad_out, routes, counts, up_weight, down_weight):
    group_rows, lanes = tokens.shape
    experts, width, hidden = up_weight.shape
    segments = routes.shape[1]
    high = lax.Precision.HIGHEST
    n_y = lax.axis_size("y")
    n_dp = n_y * lax.axis_size("c")
    n_z, n_x = lax.axis_size("z"), lax.axis_size("x")
    bf16 = jnp.bfloat16
    shape = jax.ShapeDtypeStruct
    here = jnp.stack([lax.axis_index(a).astype(jnp.int32) for a in ("z", "x")])
    routes_out = jnp.broadcast_to(routes, (n_dp,) + routes.shape[1:])
    all_routes = exchange(routes_out, DP)
    valid = (jnp.arange(group_rows, dtype=jnp.int32) < counts[0])[:, None]
    masked = jnp.where(valid, grad_out, jnp.zeros_like(grad_out))
    both = jnp.concatenate([tokens, masked], axis=0)
    both, all_routes = lax.optimization_barrier((both, all_routes))
    full = lax.all_gather(both, TENSOR)
    flat_routes = all_routes.reshape(-1, experts)
    local_up = jnp.einsum(
        "ke,edh->kdh", flat_routes, up_weight.astype(jnp.float32), precision=high
    ).astype(bf16)
    merged_up = exchange(local_up, DP).reshape(n_dp, segments, width, hidden)
    local_down = jnp.einsum(
        "ke,ehd->khd", flat_routes, down_weight.astype(jnp.float32), precision=high
    ).astype(bf16)
    merged_down = exchange(local_down, DP).reshape(n_dp, segments, hidden, width)

    slope, down_terms = local_kernel(
        pre_kernel,
        (
            shape((group_rows, hidden), jnp.float32),
            shape((n_dp, segments, hidden, width), bf16),
        ),
        0,
        full,
        merged_up,
    )
    down_terms = exchange(down_terms.reshape(-1, hidden, width), DP)
    hid, up_terms = local_kernel(
        back_kernel,
        (shape((group_rows, hidden), bf16), shape((n_dp, segments, width, hidden), bf16)),
        0,
        full,
        merged_down,
        slope,
    )
    parts = local_kernel(
        input_kernel, shape((n_x, n_z, group_rows, lanes), bf16), 1, here, hid, merged_up
    )
    right, left = start_sum(parts)
    near = second_hop(parts[0], right, left)
    up_terms, near = lax.optimization_barrier((up_terms, near))
    summed = finish_sum(near)
    down_grad = jnp.einsum(
        "ke,khd->ehd", flat_routes, down_terms.astype(jnp.float32), precision=high
    ).astype(bf16)
    down_inner = jnp.einsum(
        "khd,ehd->ke", down_terms, down_weight, preferred_element_type=jnp.float32
    )
    up_terms = exchange(up_terms.reshape(-1, width, hidden), DP)
    up_terms, down_grad, down_inner, summed = lax.optimization_barrier(
        (up_terms, down_grad, down_inner, summed)
    )
    up_grad = jnp.einsum(
        "ke,kdh->edh", flat_routes, up_terms.astype(jnp.float32), precision=high
    ).astype(bf16)
    inner = down_inner + jnp.einsum(
        "kdh,edh->ke", up_terms, up_weight, preferred_element_type=jnp.float32
    )
    own = jnp.sum(exchange(inner.reshape(all_routes.shape), DP), axis=0)
    pieces = exchange(jnp.broadcast_to(own[None], (n_z * n_x,) + own.shape), TENSOR)
    route_grad = jnp.sum(pieces, axis=0)[None]
    return (summed, up_grad, down_grad, route_grad)


def solution(mesh):
    fine = Mesh(mesh.devices.reshape(8, 2, 8, 4), DP + TENSOR)
    return jax.shard_map(
        body,
        mesh=fine,
        in_specs=(
            P(DP, TENSOR),
            P(DP, TENSOR),
            P(DP, None, None),
            P(DP),
            P(None, DP, TENSOR),
            P(None, TENSOR, DP),
        ),
        out_specs=(
            P(DP, TENSOR),
            P(None, DP, TENSOR),
            P(None, TENSOR, DP),
            P(DP, None, None),
        ),
        check_vma=False,
    )
```

```python
import functools

import jax
import jax.numpy as jnp
from jax import lax
from jax.experimental import pallas as pl
from jax.experimental.pallas import tpu as pltpu
from jax.sharding import Mesh, PartitionSpec as P

gelu_scale = 0.7978845608
gelu_cubic = 0.044715

DP = ("y", "c")
TENSOR = ("z", "x")


def gelu_pair(inputs):
    inner = gelu_scale * (inputs + gelu_cubic * inputs * inputs * inputs)
    tangent = jnp.tanh(inner)
    activated = 0.5 * inputs * (1.0 + tangent)
    derivative = 0.5 * (1.0 + tangent) + 0.5 * inputs * (1.0 - tangent * tangent) * gelu_scale * (
        1.0 + 3.0 * gelu_cubic * inputs * inputs
    )
    return (activated, derivative)


def dot(lhs, rhs, lhs_dim, rhs_dim):
    return lax.dot_general(
        lhs, rhs, (((lhs_dim,), (rhs_dim,)), ((), ())), preferred_element_type=jnp.float32
    )


def vmem(count):
    return [pl.BlockSpec(memory_space=pltpu.VMEM) for _ in range(count)]


def local_kernel(kernel, out_shapes, scalars, *args):
    smem = [pl.BlockSpec(memory_space=pltpu.SMEM) for _ in range(scalars)]
    return pl.pallas_call(
        kernel,
        out_shape=out_shapes,
        in_specs=smem + vmem(len(args) - scalars),
        out_specs=jax.tree.map(lambda _: vmem(1)[0], out_shapes),
        compiler_params=pltpu.CompilerParams(vmem_limit_bytes=56 * 1024 * 1024),
    )(*args)


def pair(full_ref, i, start, rows):
    return jnp.concatenate(
        [
            full_ref[2 * i, pl.ds(start, rows), :],
            full_ref[2 * i + 1, pl.ds(start, rows), :],
        ],
        axis=1,
    )


def pre_kernel(full_ref, up_ref, slope_ref, term_ref):
    slices, segments = term_ref.shape[0], term_ref.shape[1]
    group_rows = slope_ref.shape[0]
    rows = group_rows // segments
    for s in range(segments):
        pre = jnp.zeros((rows, slope_ref.shape[1]), jnp.float32)
        for i in range(slices):
            pre = pre + dot(pair(full_ref, i, s * rows, rows), up_ref[i, s], 1, 0)
        activated, derivative = gelu_pair(pre)
        turned = activated.astype(jnp.bfloat16).T
        slope_ref[pl.ds(s * rows, rows), :] = derivative
        for i in range(slices):
            term = dot(turned, pair(full_ref, i, group_rows + s * rows, rows), 1, 0)
            for half in range(2):
                at = slice(half * 128, (half + 1) * 128)
                term_ref[i, s, at, :] = term[:, at].astype(jnp.bfloat16)


def back_kernel(full_ref, down_ref, slope_ref, hid_ref):
    slices, segments = down_ref.shape[0], down_ref.shape[1]
    group_rows, hidden = slope_ref.shape
    rows = group_rows // segments
    for s in range(segments):
        back = jnp.zeros((rows, hidden), jnp.float32)
        for i in range(slices):
            back = back + dot(pair(full_ref, i, group_rows + s * rows, rows), down_ref[i, s], 1, 1)
        hid_ref[pl.ds(s * rows, rows), :] = (
            back * slope_ref[pl.ds(s * rows, rows), :]
        ).astype(jnp.bfloat16)


def up_kernel(full_ref, hid_ref, term_ref):
    slices, segments = term_ref.shape[0], term_ref.shape[1]
    rows = hid_ref.shape[0] // segments
    for s in range(segments):
        hidden = hid_ref[pl.ds(s * rows, rows), :]
        for i in range(slices):
            term_ref[i, s] = dot(pair(full_ref, i, s * rows, rows), hidden, 0, 0).astype(
                jnp.bfloat16
            )


def input_kernel(where_ref, hid_ref, up_ref, out_ref):
    slices, segments = up_ref.shape[0], up_ref.shape[1]
    n_x, n_z, group_rows = out_ref.shape[0], out_ref.shape[1], out_ref.shape[2]
    rows = group_rows // segments
    z, x = where_ref[0], where_ref[1]
    for s in range(segments):
        hidden = hid_ref[pl.ds(s * rows, rows), :]
        for i in range(slices):
            part = dot(hidden, up_ref[i, s], 1, 1).astype(jnp.bfloat16)
            for half in range(2):
                t = 2 * i + half
                to_x = lax.rem(t % n_x - x + n_x, n_x)
                to_z = lax.rem(t // n_x - z + n_z, n_z)
                out_ref[to_x, to_z, pl.ds(s * rows, rows), :] = part[
                    :, half * 128 : (half + 1) * 128
                ]


def exchange(value, axes):
    return lax.all_to_all(value, axes, split_axis=0, concat_axis=0, tiled=True)


def shift(value, axis, by):
    size = lax.axis_size(axis)
    return lax.ppermute(value, axis, [(i, (i + by) % size) for i in range(size)])


def add(*values):
    return functools.reduce(lambda a, b: a + b, [v.astype(jnp.float32) for v in values])


def start_sum(parts):
    half = parts.shape[1] // 2
    bf16 = jnp.bfloat16
    from_left = shift(parts[2, :half], "x", 1)
    from_right = shift(parts[2, half:], "x", -1)
    right = jnp.concatenate([add(parts[1, :half], from_left).astype(bf16), parts[1, half:]])
    left = jnp.concatenate([parts[3, :half], add(parts[3, half:], from_right).astype(bf16)])
    return right, left


def second_hop(own, right, left):
    return add(own, shift(right, "x", 1), shift(left, "x", -1)).astype(jnp.bfloat16)


def finish_sum(near):
    hops = [shift(near[k], "z", k) for k in range(1, near.shape[0])]
    return add(near[0], *hops).astype(jnp.bfloat16)


def body(tokens, grad_out, routes, counts, up_weight, down_weight):
    group_rows, lanes = tokens.shape
    experts, width, hidden = up_weight.shape
    segments = routes.shape[1]
    high = lax.Precision.HIGHEST
    n_y = lax.axis_size("y")
    n_dp = n_y * lax.axis_size("c")
    n_z, n_x = lax.axis_size("z"), lax.axis_size("x")
    bf16 = jnp.bfloat16
    shape = jax.ShapeDtypeStruct
    here = jnp.stack([lax.axis_index(a).astype(jnp.int32) for a in ("z", "x")])
    routes_out = jnp.broadcast_to(routes, (n_dp,) + routes.shape[1:])
    all_routes = exchange(routes_out, DP)
    valid = (jnp.arange(group_rows, dtype=jnp.int32) < counts[0])[:, None]
    masked = jnp.where(valid, grad_out, jnp.zeros_like(grad_out))
    both = jnp.concatenate([tokens, masked], axis=0)
    both, all_routes = lax.optimization_barrier((both, all_routes))
    full = lax.all_gather(both, TENSOR)
    flat_routes = all_routes.reshape(-1, experts)
    def merge(weight):
        return jnp.einsum(
            "ke,eab->kab", flat_routes, weight.astype(jnp.float32), precision=high
        ).astype(bf16)

    merged_up = exchange(merge(up_weight), DP).reshape(n_dp, segments, width, hidden)
    merged_down = exchange(merge(down_weight), DP).reshape(n_dp, segments, hidden, width)
    down_halves = jnp.concatenate([down_weight[:, :, :lanes], down_weight[:, :, lanes:]], axis=1)
    merged_up, down_halves = lax.optimization_barrier((merged_up, down_halves))

    slope, down_terms = local_kernel(
        pre_kernel,
        (
            shape((group_rows, hidden), jnp.float32),
            shape((n_dp, segments, width, hidden), bf16),
        ),
        0,
        full,
        merged_up,
    )
    down_terms = exchange(down_terms.reshape(-1, 2 * hidden, lanes), DP)
    hid = local_kernel(
        back_kernel, shape((group_rows, hidden), bf16), 0, full, merged_down, slope
    )
    parts = local_kernel(
        input_kernel, shape((n_x, n_z, group_rows, lanes), bf16), 1, here, hid, merged_up
    )
    up_terms = local_kernel(
        up_kernel, shape((n_dp, segments, width, hidden), bf16), 0, full, hid
    )
    right, left = start_sum(parts)
    near = second_hop(parts[0], right, left)
    up_terms, near = lax.optimization_barrier((up_terms, near))
    summed = finish_sum(near)
    down_grad = jnp.einsum(
        "ke,kab->eab", flat_routes, down_terms.astype(jnp.float32), precision=high
    ).astype(bf16)
    down_grad = jnp.concatenate([down_grad[:, :hidden], down_grad[:, hidden:]], axis=2)
    down_inner = jnp.einsum(
        "kab,eab->ke", down_terms, down_halves, preferred_element_type=jnp.float32
    )
    up_terms = exchange(up_terms.reshape(-1, width, hidden), DP)
    up_terms, down_inner = lax.optimization_barrier((up_terms, down_inner))
    up_grad = jnp.einsum(
        "ke,kdh->edh", flat_routes, up_terms.astype(jnp.float32), precision=high
    ).astype(bf16)
    inner = down_inner + jnp.einsum(
        "kdh,edh->ke", up_terms, up_weight, preferred_element_type=jnp.float32
    )
    own = jnp.sum(exchange(inner.reshape(all_routes.shape), DP), axis=0)
    pieces = exchange(jnp.broadcast_to(own[None], (n_z * n_x,) + own.shape), TENSOR)
    route_grad = jnp.sum(pieces, axis=0)[None]
    return (summed, up_grad, down_grad, route_grad)


def solution(mesh):
    fine = Mesh(mesh.devices.reshape(8, 2, 8, 4), DP + TENSOR)
    return jax.shard_map(
        body,
        mesh=fine,
        in_specs=(
            P(DP, TENSOR),
            P(DP, TENSOR),
            P(DP, None, None),
            P(DP),
            P(None, DP, TENSOR),
            P(None, TENSOR, DP),
        ),
        out_specs=(
            P(DP, TENSOR),
            P(None, DP, TENSOR),
            P(None, TENSOR, DP),
            P(DP, None, None),
        ),
        check_vma=False,
    )
```

```python
import functools

import jax
import jax.numpy as jnp
from jax import lax
from jax.experimental import pallas as pl
from jax.experimental.pallas import tpu as pltpu
from jax.sharding import Mesh, PartitionSpec as P

gelu_scale = 0.7978845608
gelu_cubic = 0.044715

DP = ("y", "c")
TENSOR = ("z", "x")


def gelu_pair(inputs):
    inner = gelu_scale * (inputs + gelu_cubic * inputs * inputs * inputs)
    tangent = jnp.tanh(inner)
    activated = 0.5 * inputs * (1.0 + tangent)
    derivative = 0.5 * (1.0 + tangent) + 0.5 * inputs * (1.0 - tangent * tangent) * gelu_scale * (
        1.0 + 3.0 * gelu_cubic * inputs * inputs
    )
    return (activated, derivative)


def dot(lhs, rhs, lhs_dim, rhs_dim):
    return lax.dot_general(
        lhs, rhs, (((lhs_dim,), (rhs_dim,)), ((), ())), preferred_element_type=jnp.float32
    )


def vmem(count):
    return [pl.BlockSpec(memory_space=pltpu.VMEM) for _ in range(count)]


def local_kernel(kernel, out_shapes, scalars, *args):
    smem = [pl.BlockSpec(memory_space=pltpu.SMEM) for _ in range(scalars)]
    return pl.pallas_call(
        kernel,
        out_shape=out_shapes,
        in_specs=smem + vmem(len(args) - scalars),
        out_specs=jax.tree.map(lambda _: vmem(1)[0], out_shapes),
        compiler_params=pltpu.CompilerParams(vmem_limit_bytes=56 * 1024 * 1024),
    )(*args)


def pair(full_ref, i, start, rows):
    return jnp.concatenate(
        [
            full_ref[2 * i, pl.ds(start, rows), :],
            full_ref[2 * i + 1, pl.ds(start, rows), :],
        ],
        axis=1,
    )


def pre_kernel(full_ref, up_ref, slope_ref, term_ref):
    slices, segments = term_ref.shape[0], term_ref.shape[1]
    group_rows = slope_ref.shape[0]
    rows = group_rows // segments
    for s in range(segments):
        pre = jnp.zeros((rows, slope_ref.shape[1]), jnp.float32)
        for i in range(slices):
            pre = pre + dot(pair(full_ref, i, s * rows, rows), up_ref[i, s], 1, 0)
        activated, derivative = gelu_pair(pre)
        turned = activated.astype(jnp.bfloat16).T
        slope_ref[pl.ds(s * rows, rows), :] = derivative
        for i in range(slices):
            term = dot(turned, pair(full_ref, i, group_rows + s * rows, rows), 1, 0)
            for half in range(2):
                at = slice(half * 128, (half + 1) * 128)
                term_ref[i, s, at, :] = term[:, at].astype(jnp.bfloat16)


def back_kernel(where_ref, full_ref, slope_ref, *refs):
    downs, hid_ref = refs[:-1], refs[-1]
    n_y, segments = len(downs), downs[0].shape[1]
    group_rows, hidden = slope_ref.shape
    rows = group_rows // segments
    y, core = where_ref[2], where_ref[3]
    for s in range(segments):
        back = jnp.zeros((rows, hidden), jnp.float32)
        for k in range(n_y):
            for other in range(2):
                i = 2 * lax.rem(y - k + n_y, n_y) + (1 - core if other else core)
                grads = pair(full_ref, i, group_rows + s * rows, rows)
                back = back + dot(grads, downs[k][other, s], 1, 1)
        hid_ref[pl.ds(s * rows, rows), :] = (
            back * slope_ref[pl.ds(s * rows, rows), :]
        ).astype(jnp.bfloat16)


def up_kernel(full_ref, hid_ref, term_ref):
    slices, segments = term_ref.shape[0], term_ref.shape[1]
    rows = hid_ref.shape[0] // segments
    for s in range(segments):
        hidden = hid_ref[pl.ds(s * rows, rows), :]
        for i in range(slices):
            term_ref[i, s] = dot(pair(full_ref, i, s * rows, rows), hidden, 0, 0).astype(
                jnp.bfloat16
            )


def input_kernel(where_ref, hid_ref, up_ref, out_ref):
    slices, segments = up_ref.shape[0], up_ref.shape[1]
    n_x, n_z, group_rows = out_ref.shape[0], out_ref.shape[1], out_ref.shape[2]
    rows = group_rows // segments
    z, x = where_ref[0], where_ref[1]
    for s in range(segments):
        hidden = hid_ref[pl.ds(s * rows, rows), :]
        for i in range(slices):
            part = dot(hidden, up_ref[i, s], 1, 1).astype(jnp.bfloat16)
            for half in range(2):
                t = 2 * i + half
                to_x = lax.rem(t % n_x - x + n_x, n_x)
                to_z = lax.rem(t // n_x - z + n_z, n_z)
                out_ref[to_x, to_z, pl.ds(s * rows, rows), :] = part[
                    :, half * 128 : (half + 1) * 128
                ]


def exchange(value, axes):
    return lax.all_to_all(value, axes, split_axis=0, concat_axis=0, tiled=True)


def shift(value, axis, by):
    size = lax.axis_size(axis)
    return lax.ppermute(value, axis, [(i, (i + by) % size) for i in range(size)])


def from_here(value, dim, axis):
    twice = jnp.concatenate([value, value], axis=dim)
    return lax.dynamic_slice_in_dim(twice, lax.axis_index(axis), value.shape[dim], dim)


def add(*values):
    return functools.reduce(lambda a, b: a + b, [v.astype(jnp.float32) for v in values])


def start_sum(parts):
    half = parts.shape[1] // 2
    bf16 = jnp.bfloat16
    from_left = shift(parts[2, :half], "x", 1)
    from_right = shift(parts[2, half:], "x", -1)
    right = jnp.concatenate([add(parts[1, :half], from_left).astype(bf16), parts[1, half:]])
    left = jnp.concatenate([parts[3, :half], add(parts[3, half:], from_right).astype(bf16)])
    return right, left


def second_hop(own, right, left):
    return add(own, shift(right, "x", 1), shift(left, "x", -1)).astype(jnp.bfloat16)


def finish_sum(near):
    hops = [shift(near[k], "z", k) for k in range(1, near.shape[0])]
    return add(near[0], *hops).astype(jnp.bfloat16)


def body(tokens, grad_out, routes, counts, up_weight, down_weight):
    group_rows, lanes = tokens.shape
    experts, width, hidden = up_weight.shape
    segments = routes.shape[1]
    high = lax.Precision.HIGHEST
    n_y = lax.axis_size("y")
    n_dp = n_y * lax.axis_size("c")
    n_z, n_x = lax.axis_size("z"), lax.axis_size("x")
    bf16 = jnp.bfloat16
    shape = jax.ShapeDtypeStruct
    here = jnp.stack([lax.axis_index(a).astype(jnp.int32) for a in ("z", "x", "y", "c")])
    routes_out = jnp.broadcast_to(routes, (n_dp,) + routes.shape[1:])
    all_routes = exchange(routes_out, DP)
    valid = (jnp.arange(group_rows, dtype=jnp.int32) < counts[0])[:, None]
    masked = jnp.where(valid, grad_out, jnp.zeros_like(grad_out))
    both = jnp.concatenate([tokens, masked], axis=0)
    full = lax.all_gather(both, TENSOR)
    flat_routes = all_routes.reshape(-1, experts)
    def merge(rows, weight):
        return jnp.einsum(
            "ke,eab->kab", rows, weight.astype(jnp.float32), precision=high
        ).astype(bf16)

    merged_up = exchange(merge(flat_routes, up_weight), DP)
    merged_up = merged_up.reshape(n_dp, segments, width, hidden)
    turned_routes = from_here(from_here(all_routes.reshape(n_y, 2, segments, experts), 0, "y"), 1, "c")
    local_down = merge(turned_routes.swapaxes(0, 1).reshape(-1, experts), down_weight)
    local_down = local_down.reshape(2, n_y, segments, hidden, width)
    crossed = shift(local_down[1], "c", 1)
    downs = []
    for k in range(n_y):
        out = jnp.stack([local_down[0, k], crossed[k]])
        downs.append(shift(out, "y", k) if k else out)
    down_halves = jnp.concatenate([down_weight[:, :, :lanes], down_weight[:, :, lanes:]], axis=1)
    merged_up, down_halves = lax.optimization_barrier((merged_up, down_halves))

    slope, down_terms = local_kernel(
        pre_kernel,
        (
            shape((group_rows, hidden), jnp.float32),
            shape((n_dp, segments, width, hidden), bf16),
        ),
        0,
        full,
        merged_up,
    )
    down_terms, *downs = lax.optimization_barrier((down_terms, *downs))
    down_terms = exchange(down_terms.reshape(-1, 2 * hidden, lanes), DP)
    hid = local_kernel(
        back_kernel, shape((group_rows, hidden), bf16), 1, here, full, slope, *downs
    )
    parts = local_kernel(
        input_kernel, shape((n_x, n_z, group_rows, lanes), bf16), 1, here, hid, merged_up
    )
    up_terms = local_kernel(
        up_kernel, shape((n_dp, segments, width, hidden), bf16), 0, full, hid
    )
    right, left = start_sum(parts)
    near = second_hop(parts[0], right, left)
    up_terms, near = lax.optimization_barrier((up_terms, near))
    summed = finish_sum(near)
    down_grad = jnp.einsum(
        "ke,kab->eab", flat_routes, down_terms.astype(jnp.float32), precision=high
    ).astype(bf16)
    down_grad = jnp.concatenate([down_grad[:, :hidden], down_grad[:, hidden:]], axis=2)
    down_inner = jnp.einsum(
        "kab,eab->ke", down_terms, down_halves, preferred_element_type=jnp.float32
    )
    up_terms = exchange(up_terms.reshape(-1, width, hidden), DP)
    up_terms, down_inner = lax.optimization_barrier((up_terms, down_inner))
    up_grad = jnp.einsum(
        "ke,kdh->edh", flat_routes, up_terms.astype(jnp.float32), precision=high
    ).astype(bf16)
    inner = down_inner + jnp.einsum(
        "kdh,edh->ke", up_terms, up_weight, preferred_element_type=jnp.float32
    )
    own = jnp.sum(exchange(inner.reshape(all_routes.shape), DP), axis=0)
    pieces = exchange(jnp.broadcast_to(own[None], (n_z * n_x,) + own.shape), TENSOR)
    route_grad = jnp.sum(pieces, axis=0)[None]
    return (summed, up_grad, down_grad, route_grad)


def solution(mesh):
    fine = Mesh(mesh.devices.reshape(8, 2, 8, 4), DP + TENSOR)
    return jax.shard_map(
        body,
        mesh=fine,
        in_specs=(
            P(DP, TENSOR),
            P(DP, TENSOR),
            P(DP, None, None),
            P(DP),
            P(None, DP, TENSOR),
            P(None, TENSOR, DP),
        ),
        out_specs=(
            P(DP, TENSOR),
            P(None, DP, TENSOR),
            P(None, TENSOR, DP),
            P(DP, None, None),
        ),
        check_vma=False,
    )
```

```python
import functools

import jax
import jax.numpy as jnp
from jax import lax
from jax.experimental import pallas as pl
from jax.experimental.pallas import tpu as pltpu
from jax.sharding import Mesh, PartitionSpec as P

gelu_scale = 0.7978845608
gelu_cubic = 0.044715

DP = ("y", "c")
TENSOR = ("z", "x")


def gelu_pair(inputs):
    inner = gelu_scale * (inputs + gelu_cubic * inputs * inputs * inputs)
    tangent = jnp.tanh(inner)
    activated = 0.5 * inputs * (1.0 + tangent)
    derivative = 0.5 * (1.0 + tangent) + 0.5 * inputs * (1.0 - tangent * tangent) * gelu_scale * (
        1.0 + 3.0 * gelu_cubic * inputs * inputs
    )
    return (activated, derivative)


def dot(lhs, rhs, lhs_dim, rhs_dim):
    return lax.dot_general(
        lhs, rhs, (((lhs_dim,), (rhs_dim,)), ((), ())), preferred_element_type=jnp.float32
    )


def vmem(count):
    return [pl.BlockSpec(memory_space=pltpu.VMEM) for _ in range(count)]


def local_kernel(kernel, out_shapes, scalars, *args):
    smem = [pl.BlockSpec(memory_space=pltpu.SMEM) for _ in range(scalars)]
    return pl.pallas_call(
        kernel,
        out_shape=out_shapes,
        in_specs=smem + vmem(len(args) - scalars),
        out_specs=jax.tree.map(lambda _: vmem(1)[0], out_shapes),
        compiler_params=pltpu.CompilerParams(vmem_limit_bytes=56 * 1024 * 1024),
    )(*args)


def pair(full_ref, i, start, rows):
    return jnp.concatenate(
        [
            full_ref[2 * i, pl.ds(start, rows), :],
            full_ref[2 * i + 1, pl.ds(start, rows), :],
        ],
        axis=1,
    )


def pre_kernel(full_ref, up_ref, slope_ref, term_ref):
    slices, segments = term_ref.shape[0], term_ref.shape[1]
    group_rows = slope_ref.shape[0]
    rows = group_rows // segments
    for s in range(segments):
        pre = jnp.zeros((rows, slope_ref.shape[1]), jnp.float32)
        for i in range(slices):
            pre = pre + dot(pair(full_ref, i, s * rows, rows), up_ref[i, s], 1, 0)
        activated, derivative = gelu_pair(pre)
        turned = activated.astype(jnp.bfloat16).T
        slope_ref[pl.ds(s * rows, rows), :] = derivative
        for i in range(slices):
            term = dot(turned, pair(full_ref, i, group_rows + s * rows, rows), 1, 0)
            for half in range(2):
                at = slice(half * 128, (half + 1) * 128)
                term_ref[i, s, at, :] = term[:, at].astype(jnp.bfloat16)


def back_kernel(order, where_ref, full_ref, slope_ref, *refs):
    downs, hid_ref = refs[:-1], refs[-1]
    n_y, segments = len(downs), downs[0].shape[1]
    group_rows, hidden = slope_ref.shape
    rows = group_rows // segments
    y, core = where_ref[2], where_ref[3]
    for s in range(segments):
        back = jnp.zeros((rows, hidden), jnp.float32)
        for k, down_ref in zip(order, downs):
            for other in range(2):
                i = 2 * lax.rem(y - k + n_y, n_y) + (1 - core if other else core)
                grads = pair(full_ref, i, group_rows + s * rows, rows)
                back = back + dot(grads, down_ref[other, s], 1, 1)
        hid_ref[pl.ds(s * rows, rows), :] = (
            back * slope_ref[pl.ds(s * rows, rows), :]
        ).astype(jnp.bfloat16)


def up_kernel(full_ref, hid_ref, term_ref):
    slices, segments = term_ref.shape[0], term_ref.shape[1]
    rows = hid_ref.shape[0] // segments
    for s in range(segments):
        hidden = hid_ref[pl.ds(s * rows, rows), :]
        for i in range(slices):
            term_ref[i, s] = dot(pair(full_ref, i, s * rows, rows), hidden, 0, 0).astype(
                jnp.bfloat16
            )


def input_kernel(where_ref, hid_ref, up_ref, out_ref):
    slices, segments = up_ref.shape[0], up_ref.shape[1]
    n_x, n_z, group_rows = out_ref.shape[0], out_ref.shape[1], out_ref.shape[2]
    rows = group_rows // segments
    z, x = where_ref[0], where_ref[1]
    for s in range(segments):
        hidden = hid_ref[pl.ds(s * rows, rows), :]
        for i in range(slices):
            part = dot(hidden, up_ref[i, s], 1, 1).astype(jnp.bfloat16)
            for half in range(2):
                t = 2 * i + half
                to_x = lax.rem(t % n_x - x + n_x, n_x)
                to_z = lax.rem(t // n_x - z + n_z, n_z)
                out_ref[to_x, to_z, pl.ds(s * rows, rows), :] = part[
                    :, half * 128 : (half + 1) * 128
                ]


def exchange(value, axes):
    return lax.all_to_all(value, axes, split_axis=0, concat_axis=0, tiled=True)


def shift(value, axis, by):
    size = lax.axis_size(axis)
    return lax.ppermute(value, axis, [(i, (i + by) % size) for i in range(size)])


def from_here(value, dim, axis):
    twice = jnp.concatenate([value, value], axis=dim)
    return lax.dynamic_slice_in_dim(twice, lax.axis_index(axis), value.shape[dim], dim)


def add(*values):
    return functools.reduce(lambda a, b: a + b, [v.astype(jnp.float32) for v in values])


def start_sum(parts):
    half = parts.shape[1] // 2
    bf16 = jnp.bfloat16
    from_left = shift(parts[2, :half], "x", 1)
    from_right = shift(parts[2, half:], "x", -1)
    right = jnp.concatenate([add(parts[1, :half], from_left).astype(bf16), parts[1, half:]])
    left = jnp.concatenate([parts[3, :half], add(parts[3, half:], from_right).astype(bf16)])
    return right, left


def finish_sum(own, from_left, from_right):
    bf16 = jnp.bfloat16
    near = add(own, from_left, from_right).astype(bf16)
    near = near.reshape((near.shape[0] // 2, 2) + near.shape[1:])
    hops = [shift(near[k], "z", 2 * k) for k in range(1, near.shape[0])]
    near = add(near[0], *hops).astype(bf16)
    return add(near[0], shift(near[1], "z", 1)).astype(bf16)


def body(tokens, grad_out, routes, counts, up_weight, down_weight):
    group_rows, lanes = tokens.shape
    experts, width, hidden = up_weight.shape
    segments = routes.shape[1]
    high = lax.Precision.HIGHEST
    n_y = lax.axis_size("y")
    n_dp = n_y * lax.axis_size("c")
    n_z, n_x = lax.axis_size("z"), lax.axis_size("x")
    bf16 = jnp.bfloat16
    shape = jax.ShapeDtypeStruct
    here = jnp.stack([lax.axis_index(a).astype(jnp.int32) for a in ("z", "x", "y", "c")])
    routes_out = jnp.broadcast_to(routes, (n_dp,) + routes.shape[1:])
    all_routes = exchange(routes_out, DP)
    valid = (jnp.arange(group_rows, dtype=jnp.int32) < counts[0])[:, None]
    masked = jnp.where(valid, grad_out, jnp.zeros_like(grad_out))
    both = jnp.concatenate([tokens, masked], axis=0)
    full = lax.all_gather(both, TENSOR)
    flat_routes = all_routes.reshape(-1, experts)
    def merge(rows, weight):
        return jnp.einsum(
            "ke,eab->kab", rows, weight.astype(jnp.float32), precision=high
        ).astype(bf16)

    merged_up = exchange(merge(flat_routes, up_weight), DP)
    merged_up = merged_up.reshape(n_dp, segments, width, hidden)
    turned_routes = from_here(from_here(all_routes.reshape(n_y, 2, segments, experts), 0, "y"), 1, "c")
    local_down = merge(turned_routes.swapaxes(0, 1).reshape(-1, experts), down_weight)
    local_down = local_down.reshape(2, n_y, segments, hidden, width)
    crossed = shift(local_down[1], "c", 1)
    order = sorted(range(n_y), key=lambda k: abs(2 * k - n_y))
    downs = [jnp.stack([local_down[0, k], crossed[k]]) for k in order]
    downs = [shift(out, "y", k) if k else out for k, out in zip(order, downs)]
    down_halves = jnp.concatenate([down_weight[:, :, :lanes], down_weight[:, :, lanes:]], axis=1)
    merged_up, down_halves = lax.optimization_barrier((merged_up, down_halves))

    slope, down_terms = local_kernel(
        pre_kernel,
        (
            shape((group_rows, hidden), jnp.float32),
            shape((n_dp, segments, width, hidden), bf16),
        ),
        0,
        full,
        merged_up,
    )
    down_terms, *downs = lax.optimization_barrier((down_terms, *downs))
    down_terms = exchange(down_terms.reshape(-1, 2 * hidden, lanes), DP)
    hid = local_kernel(
        functools.partial(back_kernel, order),
        shape((group_rows, hidden), bf16),
        1,
        here,
        full,
        slope,
        *downs,
    )
    parts = local_kernel(
        input_kernel, shape((n_x, n_z, group_rows, lanes), bf16), 1, here, hid, merged_up
    )
    up_terms = local_kernel(
        up_kernel, shape((n_dp, segments, width, hidden), bf16), 0, full, hid
    )
    right, left = start_sum(parts)
    from_left, from_right = shift(right, "x", 1), shift(left, "x", -1)
    up_terms, from_left, from_right = lax.optimization_barrier((up_terms, from_left, from_right))
    summed = finish_sum(parts[0], from_left, from_right)
    down_grad = jnp.einsum(
        "ke,kab->eab", flat_routes, down_terms.astype(jnp.float32), precision=high
    ).astype(bf16)
    down_grad = jnp.concatenate([down_grad[:, :hidden], down_grad[:, hidden:]], axis=2)
    down_inner = jnp.einsum(
        "kab,eab->ke", down_terms, down_halves, preferred_element_type=jnp.float32
    )
    up_terms = exchange(up_terms.reshape(-1, width, hidden), DP)
    up_terms, down_inner = lax.optimization_barrier((up_terms, down_inner))
    up_grad = jnp.einsum(
        "ke,kdh->edh", flat_routes, up_terms.astype(jnp.float32), precision=high
    ).astype(bf16)
    inner = down_inner + jnp.einsum(
        "kdh,edh->ke", up_terms, up_weight, preferred_element_type=jnp.float32
    )
    own = jnp.sum(exchange(inner.reshape(all_routes.shape), DP), axis=0)
    pieces = exchange(jnp.broadcast_to(own[None], (n_z * n_x,) + own.shape), TENSOR)
    route_grad = jnp.sum(pieces, axis=0)[None]
    return (summed, up_grad, down_grad, route_grad)


def solution(mesh):
    fine = Mesh(mesh.devices.reshape(8, 2, 8, 4), DP + TENSOR)
    return jax.shard_map(
        body,
        mesh=fine,
        in_specs=(
            P(DP, TENSOR),
            P(DP, TENSOR),
            P(DP, None, None),
            P(DP),
            P(None, DP, TENSOR),
            P(None, TENSOR, DP),
        ),
        out_specs=(
            P(DP, TENSOR),
            P(None, DP, TENSOR),
            P(None, TENSOR, DP),
            P(DP, None, None),
        ),
        check_vma=False,
    )
```

```python
import functools

import jax
import jax.numpy as jnp
from jax import lax
from jax.experimental import pallas as pl
from jax.experimental.pallas import tpu as pltpu
from jax.sharding import Mesh, PartitionSpec as P

gelu_scale = 0.7978845608
gelu_cubic = 0.044715

DP = ("y", "c")
TENSOR = ("z", "x")


def gelu_pair(inputs):
    inner = gelu_scale * (inputs + gelu_cubic * inputs * inputs * inputs)
    tangent = jnp.tanh(inner)
    activated = 0.5 * inputs * (1.0 + tangent)
    derivative = 0.5 * (1.0 + tangent) + 0.5 * inputs * (1.0 - tangent * tangent) * gelu_scale * (
        1.0 + 3.0 * gelu_cubic * inputs * inputs
    )
    return (activated, derivative)


def dot(lhs, rhs, lhs_dim, rhs_dim):
    return lax.dot_general(
        lhs, rhs, (((lhs_dim,), (rhs_dim,)), ((), ())), preferred_element_type=jnp.float32
    )


def vmem(count):
    return [pl.BlockSpec(memory_space=pltpu.VMEM) for _ in range(count)]


def local_kernel(kernel, out_shapes, scalars, *args):
    smem = [pl.BlockSpec(memory_space=pltpu.SMEM) for _ in range(scalars)]
    return pl.pallas_call(
        kernel,
        out_shape=out_shapes,
        in_specs=smem + vmem(len(args) - scalars),
        out_specs=jax.tree.map(lambda _: vmem(1)[0], out_shapes),
        compiler_params=pltpu.CompilerParams(vmem_limit_bytes=56 * 1024 * 1024),
    )(*args)


def pair(full_ref, i, start, rows):
    return jnp.concatenate(
        [
            full_ref[2 * i, pl.ds(start, rows), :],
            full_ref[2 * i + 1, pl.ds(start, rows), :],
        ],
        axis=1,
    )


def pre_kernel(full_ref, up_ref, slope_ref, term_ref):
    slices, segments = term_ref.shape[0], term_ref.shape[1]
    group_rows = slope_ref.shape[0]
    rows = group_rows // segments
    for s in range(segments):
        pre = jnp.zeros((rows, slope_ref.shape[1]), jnp.float32)
        for i in range(slices):
            pre = pre + dot(pair(full_ref, i, s * rows, rows), up_ref[i, s], 1, 0)
        activated, derivative = gelu_pair(pre)
        turned = activated.astype(jnp.bfloat16).T
        slope_ref[pl.ds(s * rows, rows), :] = derivative
        for i in range(slices):
            term = dot(turned, pair(full_ref, i, group_rows + s * rows, rows), 1, 0)
            for half in range(2):
                at = slice(half * 128, (half + 1) * 128)
                term_ref[i, s, at, :] = term[:, at].astype(jnp.bfloat16)


def back_kernel(where_ref, full_ref, slope_ref, *refs):
    downs, hid_ref = refs[:-1], refs[-1]
    n_y, segments = len(downs), downs[0].shape[1]
    group_rows, hidden = slope_ref.shape
    rows = group_rows // segments
    y, core = where_ref[2], where_ref[3]
    for s in range(segments):
        back = jnp.zeros((rows, hidden), jnp.float32)
        for k in range(n_y):
            for other in range(2):
                i = 2 * lax.rem(y - k + n_y, n_y) + (1 - core if other else core)
                grads = pair(full_ref, i, group_rows + s * rows, rows)
                back = back + dot(grads, downs[k][other, s], 1, 1)
        hid_ref[pl.ds(s * rows, rows), :] = (
            back * slope_ref[pl.ds(s * rows, rows), :]
        ).astype(jnp.bfloat16)


def up_kernel(where_ref, full_ref, hid_ref, term_ref):
    n_y, segments = term_ref.shape[1], term_ref.shape[2]
    rows = hid_ref.shape[0] // segments
    y, core = where_ref[2], where_ref[3]
    for s in range(segments):
        hidden = hid_ref[pl.ds(s * rows, rows), :]
        for i in range(2 * n_y):
            to_y = lax.rem(i // 2 - y + n_y, n_y)
            term = dot(pair(full_ref, i, s * rows, rows), hidden, 0, 0)
            term_ref[lax.rem(i % 2 + core, 2), to_y, s] = term.astype(jnp.bfloat16)


def input_kernel(where_ref, hid_ref, up_ref, out_ref):
    slices, segments = up_ref.shape[0], up_ref.shape[1]
    n_x, n_z, group_rows = out_ref.shape[0], out_ref.shape[1], out_ref.shape[2]
    rows = group_rows // segments
    z, x = where_ref[0], where_ref[1]
    for s in range(segments):
        hidden = hid_ref[pl.ds(s * rows, rows), :]
        for i in range(slices):
            part = dot(hidden, up_ref[i, s], 1, 1).astype(jnp.bfloat16)
            for half in range(2):
                t = 2 * i + half
                to_x = lax.rem(t % n_x - x + n_x, n_x)
                to_z = lax.rem(t // n_x - z + n_z, n_z)
                out_ref[to_x, to_z, pl.ds(s * rows, rows), :] = part[
                    :, half * 128 : (half + 1) * 128
                ]


def exchange(value, axes):
    return lax.all_to_all(value, axes, split_axis=0, concat_axis=0, tiled=True)


def shift(value, axis, by):
    size = lax.axis_size(axis)
    return lax.ppermute(value, axis, [(i, (i + by) % size) for i in range(size)])


def from_here(value, dim, axis):
    twice = jnp.concatenate([value, value], axis=dim)
    return lax.dynamic_slice_in_dim(twice, lax.axis_index(axis), value.shape[dim], dim)


def backwards(value):
    return jnp.concatenate([value[:1], jnp.flip(value[1:], 0)], axis=0)


def placing(n_y, segments):
    rows = 2 * n_y * segments
    a = lax.broadcasted_iota(jnp.int32, (rows, rows), 0)
    b = lax.broadcasted_iota(jnp.int32, (rows, rows), 1)
    y, c = lax.axis_index("y"), lax.axis_index("c")
    at_y = (y - b // (2 * segments) + n_y) % n_y == a // (2 * segments)
    at_c = (b // segments + c) % 2 == (a // segments) % 2
    return (at_y & at_c & (a % segments == b % segments)).astype(jnp.float32)


def spread(parts):
    crossed = shift(parts[1], "c", 1)
    outs = [jnp.stack([parts[0, k], crossed[k]]) for k in range(parts.shape[1])]
    return [shift(out, "y", k) if k else out for k, out in enumerate(outs)]


def add(*values):
    return functools.reduce(lambda a, b: a + b, [v.astype(jnp.float32) for v in values])


def start_sum(parts):
    half = parts.shape[1] // 2
    bf16 = jnp.bfloat16
    from_left = shift(parts[2, :half], "x", 1)
    from_right = shift(parts[2, half:], "x", -1)
    right = jnp.concatenate([add(parts[1, :half], from_left).astype(bf16), parts[1, half:]])
    left = jnp.concatenate([parts[3, :half], add(parts[3, half:], from_right).astype(bf16)])
    return right, left


def second_hop(own, right, left):
    return add(own, shift(right, "x", 1), shift(left, "x", -1)).astype(jnp.bfloat16)


def finish_sum(near):
    bf16 = jnp.bfloat16
    near = near.reshape((near.shape[0] // 2, 2) + near.shape[1:])
    hops = [shift(near[k], "z", 2 * k) for k in range(1, near.shape[0])]
    near = add(near[0], *hops).astype(bf16)
    return add(near[0], shift(near[1], "z", 1)).astype(bf16)


def body(tokens, grad_out, routes, counts, up_weight, down_weight):
    group_rows, lanes = tokens.shape
    experts, width, hidden = up_weight.shape
    segments = routes.shape[1]
    high = lax.Precision.HIGHEST
    n_y = lax.axis_size("y")
    n_dp = n_y * lax.axis_size("c")
    n_z, n_x = lax.axis_size("z"), lax.axis_size("x")
    bf16 = jnp.bfloat16
    shape = jax.ShapeDtypeStruct
    here = jnp.stack([lax.axis_index(a).astype(jnp.int32) for a in ("z", "x", "y", "c")])
    routes_out = jnp.broadcast_to(routes, (n_dp,) + routes.shape[1:])
    all_routes = exchange(routes_out, DP)
    valid = (jnp.arange(group_rows, dtype=jnp.int32) < counts[0])[:, None]
    masked = jnp.where(valid, grad_out, jnp.zeros_like(grad_out))
    both = jnp.concatenate([tokens, masked], axis=0)
    full = lax.all_gather(both, TENSOR)
    flat_routes = all_routes.reshape(-1, experts)
    def merge(rows, weight):
        return jnp.einsum(
            "ke,eab->kab", rows, weight.astype(jnp.float32), precision=high
        ).astype(bf16)

    merged_up = exchange(merge(flat_routes, up_weight), DP)
    merged_up = merged_up.reshape(n_dp, segments, width, hidden)
    turned_routes = from_here(all_routes.reshape(n_y, 2, segments, experts), 1, "c")
    turned_routes = from_here(turned_routes, 0, "y")
    local_down = merge(turned_routes.swapaxes(0, 1).reshape(-1, experts), down_weight)
    local_down = local_down.reshape(2, n_y, segments, hidden, width)
    downs = spread(local_down)
    down_halves = jnp.concatenate([down_weight[:, :, :lanes], down_weight[:, :, lanes:]], axis=1)
    place = placing(n_y, segments)
    back_routes = backwards(turned_routes).reshape(-1, experts)
    merged_up, down_halves, place, back_routes, here = lax.optimization_barrier(
        (merged_up, down_halves, place, back_routes, here)
    )

    slope, down_terms = local_kernel(
        pre_kernel,
        (
            shape((group_rows, hidden), jnp.float32),
            shape((n_dp, segments, width, hidden), bf16),
        ),
        0,
        full,
        merged_up,
    )
    down_terms, *downs = lax.optimization_barrier((down_terms, *downs))
    down_terms = exchange(down_terms.reshape(-1, 2 * hidden, lanes), DP)
    hid = local_kernel(
        back_kernel, shape((group_rows, hidden), bf16), 1, here, full, slope, *downs
    )
    parts = local_kernel(
        input_kernel, shape((n_x, n_z, group_rows, lanes), bf16), 1, here, hid, merged_up
    )
    up_terms = local_kernel(
        up_kernel, shape((2, n_y, segments, width, hidden), bf16), 1, here, full, hid
    )
    right, left = start_sum(parts)
    near = second_hop(parts[0], right, left)
    up_terms = spread(up_terms)
    near, early, down_terms = lax.optimization_barrier((near, up_terms[: n_y // 2], down_terms))
    up_terms = jnp.stack(early + up_terms[n_y // 2 :]).reshape(-1, width, hidden)
    summed = finish_sum(near)
    down_grad = jnp.einsum(
        "ke,kab->eab", flat_routes, down_terms.astype(jnp.float32), precision=high
    ).astype(bf16)
    down_grad = jnp.concatenate([down_grad[:, :hidden], down_grad[:, hidden:]], axis=2)
    down_inner = jnp.einsum(
        "kab,eab->ke", down_terms, down_halves, preferred_element_type=jnp.float32
    )
    up_terms, down_inner = lax.optimization_barrier((up_terms, down_inner))
    up_grad = jnp.einsum(
        "ke,kdh->edh",
        back_routes,
        up_terms.astype(jnp.float32),
        precision=high,
    ).astype(bf16)
    up_inner = jnp.einsum("kdh,edh->ke", up_terms, up_weight, preferred_element_type=jnp.float32)
    inner = down_inner + jnp.einsum("ab,be->ae", place, up_inner, precision=high)
    own = jnp.sum(exchange(inner.reshape(all_routes.shape), DP), axis=0)
    pieces = exchange(jnp.broadcast_to(own[None], (n_z * n_x,) + own.shape), TENSOR)
    route_grad = jnp.sum(pieces, axis=0)[None]
    return (summed, up_grad, down_grad, route_grad)


def solution(mesh):
    fine = Mesh(mesh.devices.reshape(8, 2, 8, 4), DP + TENSOR)
    return jax.shard_map(
        body,
        mesh=fine,
        in_specs=(
            P(DP, TENSOR),
            P(DP, TENSOR),
            P(DP, None, None),
            P(DP),
            P(None, DP, TENSOR),
            P(None, TENSOR, DP),
        ),
        out_specs=(
            P(DP, TENSOR),
            P(None, DP, TENSOR),
            P(None, TENSOR, DP),
            P(DP, None, None),
        ),
        check_vma=False,
    )
```

```python
import functools

import jax
import jax.numpy as jnp
from jax import lax
from jax.experimental import pallas as pl
from jax.experimental.pallas import tpu as pltpu
from jax.sharding import Mesh, PartitionSpec as P

gelu_scale = 0.7978845608
gelu_cubic = 0.044715

DP = ("y", "c")
TENSOR = ("z", "x")


def gelu_pair(inputs):
    inner = gelu_scale * (inputs + gelu_cubic * inputs * inputs * inputs)
    tangent = jnp.tanh(inner)
    activated = 0.5 * inputs * (1.0 + tangent)
    derivative = 0.5 * (1.0 + tangent) + 0.5 * inputs * (1.0 - tangent * tangent) * gelu_scale * (
        1.0 + 3.0 * gelu_cubic * inputs * inputs
    )
    return (activated, derivative)


def dot(lhs, rhs, lhs_dim, rhs_dim):
    return lax.dot_general(
        lhs, rhs, (((lhs_dim,), (rhs_dim,)), ((), ())), preferred_element_type=jnp.float32
    )


def vmem(count):
    return [pl.BlockSpec(memory_space=pltpu.VMEM) for _ in range(count)]


def local_kernel(kernel, out_shapes, scalars, *args):
    smem = [pl.BlockSpec(memory_space=pltpu.SMEM) for _ in range(scalars)]
    return pl.pallas_call(
        kernel,
        out_shape=out_shapes,
        in_specs=smem + vmem(len(args) - scalars),
        out_specs=jax.tree.map(lambda _: vmem(1)[0], out_shapes),
        compiler_params=pltpu.CompilerParams(vmem_limit_bytes=56 * 1024 * 1024),
    )(*args)


def pair(full_ref, i, start, rows):
    return jnp.concatenate(
        [
            full_ref[2 * i, pl.ds(start, rows), :],
            full_ref[2 * i + 1, pl.ds(start, rows), :],
        ],
        axis=1,
    )


def pre_kernel(full_ref, up_ref, slope_ref, term_ref):
    slices, segments = term_ref.shape[0], term_ref.shape[1]
    group_rows = slope_ref.shape[0]
    rows = group_rows // segments
    for s in range(segments):
        pre = jnp.zeros((rows, slope_ref.shape[1]), jnp.float32)
        for i in range(slices):
            pre = pre + dot(pair(full_ref, i, s * rows, rows), up_ref[i, s], 1, 0)
        activated, derivative = gelu_pair(pre)
        turned = activated.astype(jnp.bfloat16).T
        slope_ref[pl.ds(s * rows, rows), :] = derivative
        for i in range(slices):
            term = dot(turned, pair(full_ref, i, group_rows + s * rows, rows), 1, 0)
            for half in range(2):
                at = slice(half * 128, (half + 1) * 128)
                term_ref[i, s, at, :] = term[:, at].astype(jnp.bfloat16)


def back_kernel(where_ref, full_ref, slope_ref, *refs):
    downs, hid_ref = refs[:-1], refs[-1]
    n_y, segments = len(downs), downs[0].shape[1]
    group_rows, hidden = slope_ref.shape
    rows = group_rows // segments
    y, core = where_ref[2], where_ref[3]
    for s in range(segments):
        back = jnp.zeros((rows, hidden), jnp.float32)
        for k in range(n_y):
            for other in range(2):
                i = 2 * lax.rem(y - k + n_y, n_y) + (1 - core if other else core)
                grads = pair(full_ref, i, group_rows + s * rows, rows)
                back = back + dot(grads, downs[k][other, s], 1, 1)
        hid_ref[pl.ds(s * rows, rows), :] = (
            back * slope_ref[pl.ds(s * rows, rows), :]
        ).astype(jnp.bfloat16)


def up_kernel(where_ref, full_ref, hid_ref, term_ref):
    n_y, segments = term_ref.shape[1], term_ref.shape[2]
    rows = hid_ref.shape[0] // segments
    y, core = where_ref[2], where_ref[3]
    for s in range(segments):
        hidden = hid_ref[pl.ds(s * rows, rows), :]
        for i in range(2 * n_y):
            to_y = lax.rem(i // 2 - y + n_y, n_y)
            term = dot(pair(full_ref, i, s * rows, rows), hidden, 0, 0)
            term_ref[lax.rem(i % 2 + core, 2), to_y, s] = term.astype(jnp.bfloat16)


def input_kernel(where_ref, hid_ref, up_ref, out_ref):
    slices, segments = up_ref.shape[0], up_ref.shape[1]
    n_x, n_z, group_rows = out_ref.shape[0], out_ref.shape[1], out_ref.shape[2]
    rows = group_rows // segments
    z, x = where_ref[0], where_ref[1]
    for s in range(segments):
        hidden = hid_ref[pl.ds(s * rows, rows), :]
        for i in range(slices):
            part = dot(hidden, up_ref[i, s], 1, 1).astype(jnp.bfloat16)
            for half in range(2):
                t = 2 * i + half
                to_x = lax.rem(t % n_x - x + n_x, n_x)
                to_z = lax.rem(t // n_x - z + n_z, n_z)
                out_ref[to_x, to_z, pl.ds(s * rows, rows), :] = part[
                    :, half * 128 : (half + 1) * 128
                ]


def exchange(value, axes):
    return lax.all_to_all(value, axes, split_axis=0, concat_axis=0, tiled=True)


def shift(value, axis, by):
    size = lax.axis_size(axis)
    return lax.ppermute(value, axis, [(i, (i + by) % size) for i in range(size)])


def from_here(value, dim, axis):
    twice = jnp.concatenate([value, value], axis=dim)
    return lax.dynamic_slice_in_dim(twice, lax.axis_index(axis), value.shape[dim], dim)


def backwards(value):
    return jnp.concatenate([value[:1], jnp.flip(value[1:], 0)], axis=0)


def placing(n_y, segments):
    rows = 2 * n_y * segments
    a = lax.broadcasted_iota(jnp.int32, (rows, rows), 0)
    b = lax.broadcasted_iota(jnp.int32, (rows, rows), 1)
    y, c = lax.axis_index("y"), lax.axis_index("c")
    at_y = (y - b // (2 * segments) + n_y) % n_y == a // (2 * segments)
    at_c = (b // segments + c) % 2 == (a // segments) % 2
    return (at_y & at_c & (a % segments == b % segments)).astype(jnp.float32)


def cross(parts):
    crossed = shift(parts[1], "c", 1)
    return [jnp.stack([parts[0, k], crossed[k]]) for k in range(parts.shape[1])]


def spread(outs):
    return [shift(out, "y", k) if k else out for k, out in enumerate(outs)]


def add(*values):
    return functools.reduce(lambda a, b: a + b, [v.astype(jnp.float32) for v in values])


def start_sum(parts):
    half = parts.shape[1] // 2
    bf16 = jnp.bfloat16
    from_left = shift(parts[2, :half], "x", 1)
    from_right = shift(parts[2, half:], "x", -1)
    right = jnp.concatenate([add(parts[1, :half], from_left).astype(bf16), parts[1, half:]])
    left = jnp.concatenate([parts[3, :half], add(parts[3, half:], from_right).astype(bf16)])
    return right, left


def second_hop(own, right, left):
    return add(own, shift(right, "x", 1), shift(left, "x", -1)).astype(jnp.bfloat16)


def finish_sum(near):
    bf16 = jnp.bfloat16
    near = near.reshape((near.shape[0] // 2, 2) + near.shape[1:])
    hops = [shift(near[k], "z", 2 * k) for k in range(1, near.shape[0])]
    near = add(near[0], *hops).astype(bf16)
    return add(near[0], shift(near[1], "z", 1)).astype(bf16)


def body(tokens, grad_out, routes, counts, up_weight, down_weight):
    group_rows, lanes = tokens.shape
    experts, width, hidden = up_weight.shape
    segments = routes.shape[1]
    high = lax.Precision.HIGHEST
    n_y = lax.axis_size("y")
    n_dp = n_y * lax.axis_size("c")
    n_z, n_x = lax.axis_size("z"), lax.axis_size("x")
    bf16 = jnp.bfloat16
    shape = jax.ShapeDtypeStruct
    here = jnp.stack([lax.axis_index(a).astype(jnp.int32) for a in ("z", "x", "y", "c")])
    routes_out = jnp.broadcast_to(routes, (n_dp,) + routes.shape[1:])
    all_routes = exchange(routes_out, DP)
    valid = (jnp.arange(group_rows, dtype=jnp.int32) < counts[0])[:, None]
    masked = jnp.where(valid, grad_out, jnp.zeros_like(grad_out))
    both = jnp.concatenate([tokens, masked], axis=0)
    full = lax.all_gather(both, TENSOR)
    flat_routes = all_routes.reshape(-1, experts)
    def merge(rows, weight):
        return jnp.einsum(
            "ke,eab->kab", rows, weight.astype(jnp.float32), precision=high
        ).astype(bf16)

    merged_up = exchange(merge(flat_routes, up_weight), DP)
    merged_up = merged_up.reshape(n_dp, segments, width, hidden)
    turned_routes = from_here(all_routes.reshape(n_y, 2, segments, experts), 1, "c")
    turned_routes = from_here(turned_routes, 0, "y")
    local_down = merge(turned_routes.swapaxes(0, 1).reshape(-1, experts), down_weight)
    local_down = local_down.reshape(2, n_y, segments, hidden, width)
    downs = spread(cross(local_down))
    down_halves = jnp.concatenate([down_weight[:, :, :lanes], down_weight[:, :, lanes:]], axis=1)
    place = placing(n_y, segments)
    back_routes = backwards(turned_routes).reshape(-1, experts)
    merged_up, down_halves, place, back_routes, here = lax.optimization_barrier(
        (merged_up, down_halves, place, back_routes, here)
    )

    slope, down_terms = local_kernel(
        pre_kernel,
        (
            shape((group_rows, hidden), jnp.float32),
            shape((n_dp, segments, width, hidden), bf16),
        ),
        0,
        full,
        merged_up,
    )
    down_terms, *downs = lax.optimization_barrier((down_terms, *downs))
    down_terms = exchange(down_terms.reshape(-1, 2 * hidden, lanes), DP)
    hid = local_kernel(
        back_kernel, shape((group_rows, hidden), bf16), 1, here, full, slope, *downs
    )
    parts = local_kernel(
        input_kernel, shape((n_x, n_z, group_rows, lanes), bf16), 1, here, hid, merged_up
    )
    up_terms = local_kernel(
        up_kernel, shape((2, n_y, segments, width, hidden), bf16), 1, here, full, hid
    )
    right, left = start_sum(parts)
    near = second_hop(parts[0], right, left)
    outs = cross(up_terms)
    summed = finish_sum(near)
    up_terms = jnp.stack(spread(outs)).reshape(-1, width, hidden)
    down_grad = jnp.einsum(
        "ke,kab->eab", flat_routes, down_terms.astype(jnp.float32), precision=high
    ).astype(bf16)
    down_grad = jnp.concatenate([down_grad[:, :hidden], down_grad[:, hidden:]], axis=2)
    down_inner = jnp.einsum(
        "kab,eab->ke", down_terms, down_halves, preferred_element_type=jnp.float32
    )
    up_terms, down_inner = lax.optimization_barrier((up_terms, down_inner))
    up_grad = jnp.einsum(
        "ke,kdh->edh",
        back_routes,
        up_terms.astype(jnp.float32),
        precision=high,
    ).astype(bf16)
    up_inner = jnp.einsum("kdh,edh->ke", up_terms, up_weight, preferred_element_type=jnp.float32)
    inner = down_inner + jnp.einsum("ab,be->ae", place, up_inner, precision=high)
    own = jnp.sum(exchange(inner.reshape(all_routes.shape), DP), axis=0)
    pieces = exchange(jnp.broadcast_to(own[None], (n_z * n_x,) + own.shape), TENSOR)
    route_grad = jnp.sum(pieces, axis=0)[None]
    return (summed, up_grad, down_grad, route_grad)


def solution(mesh):
    fine = Mesh(mesh.devices.reshape(8, 2, 8, 4), DP + TENSOR)
    return jax.shard_map(
        body,
        mesh=fine,
        in_specs=(
            P(DP, TENSOR),
            P(DP, TENSOR),
            P(DP, None, None),
            P(DP),
            P(None, DP, TENSOR),
            P(None, TENSOR, DP),
        ),
        out_specs=(
            P(DP, TENSOR),
            P(None, DP, TENSOR),
            P(None, TENSOR, DP),
            P(DP, None, None),
        ),
        check_vma=False,
    )
```
